32 devices in a mesh: cuts: 2 (over y), row: 4 (over z), vec: 4 (over x, core).
Axes of the slice: x: 2, y: 2, z: 4, core: 2. Of those that a mesh axis runs over, the one named last changes fastest.
Arguments:
- vectors: float32 [16384, 512], P(('cuts', 'row'), 'vec'), parts along dimension 0, may hold values from -6 to 6
- intersection: float32 [8192, 1536], P('row'), may hold values from -0.15625 to 0.15625
- factor: float32 [16384, 2048], P(('cuts', 'row')), parts along dimension 0, may hold values from -0.1875 to 0.1875
- pivot_rows: int32 [16384], P(('cuts', 'row')), parts along dimension 0, may hold values from 0 to 2047, as said below
- pivot_sizes: int32 [2048], P('cuts'), parts along dimension 0, may hold values from 1 to 2
- pivot_diag: float32 [4096], P('cuts'), parts along dimension 0, may hold values from 0.5 to 2
- pivot_off: float32 [2048], P('cuts'), parts along dimension 0, may hold values from 2.5 to 4
Outputs:
- partial_solve: float32 [16384, 512], P(('cuts', 'row'), 'vec'), parts along dimension 0
The draws below stay inside these ranges and needn't reach their ends.
There are 2 independent parts, one for each index of `cuts`. The reference program is written for one: setup_inputs(seed, part) draws one part's arguments, and reference() takes and returns one part's arrays. A program takes and returns all parts, laid end to end along the dimension named above; an argument that names none is the same for every part. Nothing has to cross between parts.
Inputs may be any that keep to these rules, and one draw needn't show every extreme that they name: `pivot_rows`: each aligned run of 2048 entries is a permutation of 0 to 2047. `pivot_sizes`: 2 marks a 2x2 pivot block on the pair of rows, 1 two 1x1 blocks.
All inputs are finite; a program needn't handle non-finite values.
Results may differ from the reference program's by a relative error of at most 0.00011.
Values sent between devices are 32-bit elements; how exact they have to be, the bound alone decides.
A program may use at most 128 MiB of HBM per device.

```python
import math
import jax
import jax.numpy as jnp
from jax import lax

VECS = 512
BS = 512
PANEL = 1024
PANELS = 2
CYC = 16
ROWS_DEV = 2048
OWNERS = 4
ORDER = 8192
SOLVED = 2048


def one_device(subkey):
    return jax.random.permutation(subkey, ROWS_DEV)


def draw_pivot_rows(key, part):
    subkeys = jax.random.split(jax.random.fold_in(key, 7), ORDER // ROWS_DEV)
    orders = jax.vmap(one_device)(subkeys)
    return orders.reshape(ORDER).astype(jnp.int32)


def plant(values, stream_key, smallest, largest):
    place = [jax.random.randint(jax.random.fold_in(stream_key, axis), (), 0, length) for axis, length in enumerate(values.shape)]
    longest = values.shape.index(max(values.shape))
    next_to = place[:longest] + [(place[longest] + 1) % values.shape[longest]] + place[longest + 1:]
    return values.at[tuple(place)].set(smallest).at[tuple(next_to)].set(largest)


def block_scale(rng, extent, cuts, low, largest):
    loudness, own = 1.0, jax.random.fold_in(rng, 6)
    for position, blocks in cuts:
        draws = jnp.exp(jax.random.uniform(jax.random.fold_in(own, position), (blocks,), jnp.float32, low / len(cuts), largest / len(cuts)))
        loudness = loudness * jnp.repeat(draws, extent[position] // blocks).reshape([-1 if axis == position else 1 for axis in range(len(extent))])
    return loudness


def centred(stream_key, shape, spread, most, pieces=(), kind=jnp.bfloat16):
    values = jax.random.normal(stream_key, shape, jnp.float32) * spread
    if len(pieces) > 0:
        values = block_scale(stream_key, shape, pieces, -0.22, 0.18) * values
    return jnp.clip(values, min=-most, max=most).astype(kind)


def setup_inputs(seed: int = 0, part: int = 0) -> dict:
    seeds = jax.random.split(jax.random.key(seed), 8)
    part_splits = jax.random.split(jax.random.fold_in(seeds[7], part), 8)
    vectors = centred(part_splits[0], (ORDER, VECS), 1.0, 6.0, ((0, 4), (1, 4)), jnp.float32)
    intersection = centred(seeds[1], (ORDER, 3 * BS), (3 * BS) ** -0.5, 0.15625, ((0, 4),), jnp.float32)
    factor = centred(part_splits[2], (ORDER, SOLVED), (SOLVED // 2) ** -0.5, 0.1875, ((0, 4),), jnp.float32)
    pivot_rows = draw_pivot_rows(jax.random.fold_in(jax.random.fold_in(seeds[7], part), 71), part)
    pivot_sizes = plant(jax.random.randint(part_splits[4], (SOLVED // 2,), 1, 3), jax.random.fold_in(part_splits[4], 1), 1, 2).astype(jnp.int32)
    pivot_diag = jnp.clip(jnp.exp(jax.random.uniform(part_splits[5], (SOLVED,), jnp.float32, math.log(0.5), math.log(2.0))), 0.5, 2.0)
    pivot_off = jnp.clip(jax.random.uniform(part_splits[6], (SOLVED // 2,), jnp.float32, 2.5, 4.0), 2.5, 4.0)
    return {"vectors": vectors, "intersection": intersection, "factor": factor, "pivot_rows": pivot_rows, "pivot_sizes": pivot_sizes, "pivot_diag": pivot_diag, "pivot_off": pivot_off}


def layout_rows(positions):
    device = positions // ROWS_DEV
    within = positions % ROWS_DEV
    return ((within // CYC * OWNERS + device) * CYC + within % CYC).astype(jnp.int32)

def band_product(intersection, padded, blocks_here):
    band_width = intersection.shape[1] // 3
    band_rows = intersection.reshape(blocks_here, band_width, 3 * band_width)
    result = jnp.zeros((blocks_here, band_width, padded.shape[1]), jnp.float32)
    for offset in range(3):
        window = padded[offset * band_width:offset * band_width + blocks_here * band_width]
        window = window.reshape(blocks_here, band_width, padded.shape[1])
        result = result + jnp.einsum('kij,kjv->kiv', band_rows[:, :, offset * band_width:(offset + 1) * band_width], window, precision=lax.Precision.HIGHEST)
    return result.reshape(blocks_here * band_width, padded.shape[1])

def scale_pivots(values, sizes_here, diag_here, off_here):
    paired = values.reshape(-1, 2, values.shape[1])
    leading = paired[:, 0]
    trailing = paired[:, 1]
    diag_lead = diag_here[0::2][:, None]
    diag_next = diag_here[1::2][:, None]
    coupling = off_here[:, None]
    determ = diag_lead * diag_next - coupling * coupling
    is_pair = (sizes_here == 2)[:, None]
    new_lead = jnp.where(is_pair, (diag_next * leading - coupling * trailing) / determ, leading / diag_lead)
    new_next = jnp.where(is_pair, (diag_lead * trailing - coupling * leading) / determ, trailing / diag_next)
    return jnp.stack([new_lead, new_next], axis=1).reshape(values.shape)

def reference(vectors, intersection, factor, pivot_rows, pivot_sizes, pivot_diag, pivot_off):
    padded = jnp.pad(vectors, ((BS, BS), (0, 0)))
    product = band_product(intersection, padded, ORDER // BS)
    positions = jnp.arange(ORDER, dtype=jnp.int32)
    mapped = layout_rows(positions)
    source = layout_rows(positions // ROWS_DEV * ROWS_DEV + pivot_rows.astype(jnp.int32))
    rhs_fac = jnp.zeros_like(product).at[mapped].set(product[source])
    lower_fac = jnp.zeros((ORDER, SOLVED), jnp.float32).at[mapped].set(factor)
    solved = []
    for panel_num in range(PANELS):
        first_row = panel_num * PANEL
        last_row = first_row + PANEL
        block_sol = jax.scipy.linalg.solve_triangular(lower_fac[first_row:last_row, first_row:last_row], rhs_fac[first_row:last_row], lower=True, unit_diagonal=True)
        update = jnp.dot(lower_fac[last_row:, first_row:last_row], block_sol, precision=lax.Precision.HIGHEST)
        rhs_fac = jnp.concatenate([rhs_fac[:last_row], rhs_fac[last_row:] - update], axis=0)
        solved.append(scale_pivots(block_sol, pivot_sizes[first_row // 2:last_row // 2], pivot_diag[first_row:last_row], pivot_off[first_row // 2:last_row // 2]))
    combined = jnp.concatenate(solved + [rhs_fac[SOLVED:]], axis=0)
    return combined[mapped]
```

```python
import functools
import math

import jax
import jax.numpy as jnp
from jax import lax
from jax.experimental import pallas as pl
from jax.experimental.pallas import tpu as pltpu
from jax.sharding import PartitionSpec as P

BS = 512
PANEL = 1024
PANELS = 2
CYC = 16
INV = 128
STEP = 256

MESH = pl.DeviceIdType.MESH
BF = jnp.bfloat16
F32 = jnp.float32


def halves(x):
    hi = x.astype(BF)
    return hi, (x - hi.astype(F32)).astype(BF)


def dot(a, b):
    return jnp.dot(a, b, preferred_element_type=F32)


def product(a_hi, a_lo, b_cat):
    n = b_cat.shape[1] // 2
    wide = dot(a_hi, b_cat)
    return wide[:, :n] + (wide[:, n:] + dot(a_lo, b_cat[:, :n]))


def mm(a, b):
    a_hi, a_lo = halves(a)
    return product(a_hi, a_lo, jnp.concatenate(halves(b), axis=1))


def invert_many(blocks):
    n = blocks[0].shape[0]
    row = lax.broadcasted_iota(jnp.int32, (n, n), 0)
    col = lax.broadcasted_iota(jnp.int32, (n, n), 1)
    strict = col < row
    eye = jnp.where(col == row, 1.0, 0.0).astype(F32)
    small = 16
    base = strict & (row // small == col // small)
    powers = [jnp.where(base, d, 0.0) for d in blocks]
    inv = [eye - m for m in powers]
    reach = 2
    while reach < small:
        powers = [mm(m, m) for m in powers]
        inv = [x + mm(x, m) for x, m in zip(inv, powers)]
        reach *= 2
    size = small
    while size < n:
        joined = strict & (row // (2 * size) == col // (2 * size)) & (row // size != col // size)
        mid = [mm(jnp.where(joined, d, 0.0), x) for d, x in zip(blocks, inv)]
        inv = [x - mm(x, m) for x, m in zip(inv, mid)]
        size *= 2
    return inv


def kernel(
    R, V, piv, vec_hbm, int_hbm, fac_hbm, out,
    ibuf, fbuf0, fbuf1, vbuf, halo, bcat, prod, reg, mine, rhs, lbuf, xhi, xlo, ybuf, ycat,
    in_sem, int_sem, fac_sem, own_sem,
    halo_s, halo_r, a2a_s, a2a_r, a2a_l, tri_s, tri_r, fwd_s, fwd_r, rhs_s, rhs_r,
):
    me = lax.axis_index("row")
    lane = lax.axis_index("vec")
    rows, cols = vbuf.shape
    nb = rows // BS
    slots = PANEL // R // CYC
    prow = slots * CYC
    per_owner = rows // R
    block_share = BS // R
    quarter = PANEL // V
    facs = (fbuf0, fbuf1)

    def quarter_of(v):
        order = []
        lo, hi = 0, V - 1
        while lo <= hi:
            order.append(lo)
            if hi > lo:
                order.append(hi)
            lo, hi = lo + 1, hi - 1
        return order[v]

    def rpeer(d):
        return lax.rem(me + d, R)

    def rfrom(d):
        return lax.rem(me + (R - d), R)

    def vpeer(d):
        return lax.rem(lane + d, V)

    vload = pltpu.make_async_copy(vec_hbm, vbuf, in_sem)
    vload.start()
    order = list(range(1, nb - 1)) + [0, nb - 1]
    iloads = {}
    for k in order:
        iloads[k] = pltpu.make_async_copy(
            int_hbm.at[pl.ds(k * BS, BS)], ibuf.at[pl.ds(k * BS, BS)], int_sem.at[k])
        iloads[k].start()

    barrier = pltpu.get_barrier_semaphore()
    for d in range(1, R):
        pl.semaphore_signal(barrier, 1, device_id={"row": rpeer(d)}, device_id_type=MESH)
    for d in range(1, V):
        pl.semaphore_signal(barrier, 1, device_id={"vec": vpeer(d)}, device_id_type=MESH)
    pl.semaphore_wait(barrier, R - 1 + V - 1)

    def halo_up():
        return pltpu.make_async_remote_copy(
            vec_hbm.at[pl.ds(rows - BS, BS)], halo.at[0], halo_s.at[0], halo_r.at[0],
            device_id={"row": rpeer(1)}, device_id_type=MESH)

    def halo_down():
        return pltpu.make_async_remote_copy(
            vec_hbm.at[pl.ds(0, BS)], halo.at[1], halo_s.at[1], halo_r.at[1],
            device_id={"row": rfrom(1)}, device_id_type=MESH)

    @pl.when(me < R - 1)
    def _():
        halo_up().start()

    @pl.when(me > 0)
    def _():
        halo_down().start()

    def tri_span(v):
        q = quarter_of(v)
        first = (q * quarter) // (R * CYC)
        return q, first, slots - first

    def tri_copy(p, v, d):
        q, first, count = tri_span(v)
        src = fac_hbm.at[pl.ds(p * slots + first, count), :, pl.ds(p * PANEL + q * quarter, quarter)]
        dst = lbuf.at[p, pl.ds(first, count), me, :, pl.ds(q * quarter, quarter)]
        return pltpu.make_async_remote_copy(
            src, dst, tri_s.at[p, d], tri_r.at[p, d],
            device_id={"row": rpeer(d)}, device_id_type=MESH)

    def tri_arrived(p, v, d):
        q, first, count = tri_span(v)
        dst = lbuf.at[p, pl.ds(first, count), rfrom(d), :, pl.ds(q * quarter, quarter)]
        return pltpu.make_async_remote_copy(
            dst, dst, tri_s.at[p, d], tri_r.at[p, d],
            device_id={"row": rpeer(d)}, device_id_type=MESH)

    def fwd_copy(p, v, d, w):
        q, first, count = tri_span(v)
        ref = lbuf.at[p, pl.ds(first, count), rfrom(d), :, pl.ds(q * quarter, quarter)]
        return pltpu.make_async_remote_copy(
            ref, ref, fwd_s.at[p, d, w], fwd_r.at[p, d, v],
            device_id={"vec": (v + w) % V}, device_id_type=MESH)

    def per_lane(fn):
        for v in range(V):
            @pl.when(lane == v)
            def _():
                fn(v)

    def tri_start(p):
        def go(v):
            for d in range(1, R):
                tri_copy(p, v, d).start()
        per_lane(go)

    def tri_forward(p):
        def go(v):
            for d in range(1, R):
                tri_arrived(p, v, d).wait_recv()
                for w in range(1, V):
                    fwd_copy(p, v, d, w).start()
        per_lane(go)

    def tri_wait(p):
        def go(v):
            for d in range(1, R):
                for w in range(1, V):
                    fwd_copy(p, (v + w) % V, d, 1).wait_recv()
        per_lane(go)

    def tri_drain(p):
        def go(v):
            for d in range(1, R):
                tri_copy(p, v, d).wait_send()
                for w in range(1, V):
                    fwd_copy(p, v, d, w).wait_send()
        per_lane(go)

    tri_start(0)

    owns = []
    for p in range(PANELS):
        c = pltpu.make_async_copy(
            fac_hbm.at[pl.ds(p * slots, slots), :, pl.ds(p * PANEL, PANEL)],
            lbuf.at[p, :, me], own_sem.at[p])
        c.start()
        owns.append(c)
    floads = []
    for p in range(PANELS):
        first = (p + 1) * slots
        c = pltpu.make_async_copy(
            fac_hbm.at[pl.ds(first, rows // CYC - first), :, pl.ds(p * PANEL, PANEL)],
            facs[p], fac_sem.at[p])
        c.start()
        floads.append(c)

    def put_cat(at, value):
        hi, lo = halves(value)
        bcat[at : at + value.shape[0], :cols] = hi
        bcat[at : at + value.shape[0], cols:] = lo

    vload.wait()
    for k in range(nb):
        put_cat(BS + k * BS, vbuf[k * BS : (k + 1) * BS])

    tile = STEP

    def a2a_copy(k, d):
        return pltpu.make_async_remote_copy(
            prod.at[rpeer(d), pl.ds(k * block_share, block_share)],
            reg.at[pl.ds(me * per_owner + k * block_share, block_share)],
            a2a_s.at[k, d], a2a_r.at[k, d],
            device_id={"row": rpeer(d)}, device_id_type=MESH)

    def a2a_own(k):
        return pltpu.make_async_copy(
            prod.at[me, pl.ds(k * block_share, block_share)],
            reg.at[pl.ds(me * per_owner + k * block_share, block_share)],
            a2a_l.at[k])

    def a2a_arrived(k, d):
        return pltpu.make_async_remote_copy(
            prod.at[rpeer(d), pl.ds(k * block_share, block_share)],
            reg.at[pl.ds(rfrom(d) * per_owner + k * block_share, block_share)],
            a2a_s.at[k, d], a2a_r.at[k, d],
            device_id={"row": rpeer(d)}, device_id_type=MESH)

    def band(k):
        iloads_wait(k)
        window = bcat[pl.ds(pl.multiple_of(k * BS, BS), 3 * BS), :]
        for t in range(0, BS, tile):
            a = ibuf[pl.ds(pl.multiple_of(k * BS + t, tile), tile), :]
            a_hi, a_lo = halves(a)
            value = product(a_hi, a_lo, window)
            for g in range(tile // CYC):
                number = t // CYC + g
                owner, slot = number % R, number // R
                at = pl.multiple_of(k * block_share + slot * CYC, CYC)
                prod[owner, pl.ds(at, CYC), :] = value[g * CYC : (g + 1) * CYC]
        for d in range(1, R):
            a2a_copy(k, d).start()
        a2a_own(k).start()

    def iloads_wait(k):
        at = pl.multiple_of(k * BS, BS)
        pltpu.make_async_copy(
            int_hbm.at[pl.ds(at, BS)], ibuf.at[pl.ds(at, BS)], int_sem.at[k]).wait()

    pl.loop(1, nb - 1)(band)

    @pl.when(me > 0)
    def _():
        halo_up().wait_recv()
        put_cat(0, halo[0])

    @pl.when(me == 0)
    def _():
        bcat[0:BS, :] = jnp.zeros((BS, 2 * cols), BF)

    @pl.when(me < R - 1)
    def _():
        halo_down().wait_recv()
        put_cat(BS + rows, halo[1])

    @pl.when(me == R - 1)
    def _():
        bcat[BS + rows : 2 * BS + rows, :] = jnp.zeros((BS, 2 * cols), BF)

    @pl.loop(0, 2)
    def _(i):
        band(i * (nb - 1))

    tri_forward(0)

    def lrows(p, at, count, c0, c1):
        span = R * CYC
        if count % span == 0:
            value = lbuf[p, at // span : (at + count) // span, :, :, c0:c1]
        else:
            first = at % span // CYC
            value = lbuf[p, at // span, first : first + count // CYC, :, c0:c1]
        return value.reshape(count, c1 - c0)

    def invert(p):
        for i in range(0, PANEL // STEP, 2):
            blocks = []
            for j in (i, i + 1):
                for h in range(STEP // INV):
                    at = j * STEP + h * INV
                    blocks.append(lrows(p, j * STEP, STEP, at, at + INV)[h * INV : (h + 1) * INV])
            inv = invert_many(blocks)
            for n, j in enumerate((i, i + 1)):
                first, second = inv[2 * n], inv[2 * n + 1]
                corner = lrows(p, j * STEP, STEP, j * STEP, j * STEP + INV)[INV:]
                corner = -mm(second, mm(corner, first))
                for (r0, c0), value in (((0, 0), first), ((INV, 0), corner), ((INV, INV), second)):
                    hi, lo = halves(value)
                    xhi[j, r0 : r0 + INV, c0 : c0 + INV] = hi
                    xlo[j, r0 : r0 + INV, c0 : c0 + INV] = lo
                xhi[j, 0:INV, INV:STEP] = jnp.zeros((INV, INV), BF)
                xlo[j, 0:INV, INV:STEP] = jnp.zeros((INV, INV), BF)

    def pivot(first, count, store):
        @pl.loop(0, count // 8)
        def _(i):
            picked = [reg[pl.ds(piv[first + i * 8 + j], 1), :] for j in range(8)]
            store(i, jnp.concatenate(picked, axis=0))

    def rhs_copy(p, d):
        return pltpu.make_async_remote_copy(
            mine.at[p], rhs.at[p, :, me], rhs_s.at[p, d], rhs_r.at[p, d],
            device_id={"row": rpeer(d)}, device_id_type=MESH)

    def rhs_arrived(p, d):
        return pltpu.make_async_remote_copy(
            mine.at[p], rhs.at[p, :, rfrom(d)], rhs_s.at[p, d], rhs_r.at[p, d],
            device_id={"row": rpeer(d)}, device_id_type=MESH)

    def send_rhs(p):
        for d in range(1, R):
            rhs_copy(p, d).start()
        rhs[p, :, pl.ds(me, 1)] = mine[p].reshape(slots, 1, CYC, cols)

    def blockrows(ref, p, at, count):
        span = R * CYC
        if count % span == 0:
            return ref.at[p, at // span : (at + count) // span]
        first = at % span // CYC
        return ref.at[p, at // span, first : first + count // CYC]

    def solve(p):
        for i in range(PANEL // STEP):
            at = i * STEP
            acc = blockrows(rhs, p, at, STEP)[...].reshape(STEP, cols)
            if i > 0:
                l_hi, l_lo = halves(lrows(p, at, STEP, 0, at))
                acc = acc - product(l_hi, l_lo, ycat[:at])
            y = product(xhi[i], xlo[i], jnp.concatenate(halves(acc), axis=1))
            target = blockrows(ybuf, p, at, STEP)
            target[...] = y.reshape(target.shape)
            hi, lo = halves(y)
            ycat[at : at + STEP, :cols] = hi
            ycat[at : at + STEP, cols:] = lo
        out[p * prow : (p + 1) * prow, :] = ybuf[p, :, pl.ds(me, 1)].reshape(prow, cols)

    rest = rows - PANELS * prow
    part = math.gcd(rest, STEP)

    def update_rest(p):
        f = facs[p]
        skip = (rows - (p + 1) * prow - rest) // CYC

        @pl.loop(0, rest // part)
        def _(t):
            at = pl.multiple_of(PANELS * prow + t * part, CYC)
            a = f[pl.ds(skip + t * (part // CYC), part // CYC)].reshape(part, PANEL)
            a_hi, a_lo = halves(a)
            out[pl.ds(at, part), :] = out[pl.ds(at, part), :] - product(a_hi, a_lo, ycat[...])

    owns[0].wait()
    tri_wait(0)
    invert(0)

    for k in range(nb):
        for d in range(1, R):
            a2a_arrived(k, d).wait_recv()
        a2a_own(k).wait()

    def to_mine(p):
        def store(i, value):
            mine[p, i // 2, pl.ds(pl.multiple_of(i % 2 * 8, 8), 8), :] = value
        return store

    pivot(0, prow, to_mine(0))
    send_rhs(0)
    tri_start(1)

    def to_out(i, value):
        out[pl.ds(pl.multiple_of(PANELS * prow + i * 8, 8), 8), :] = value

    pivot(PANELS * prow, rest, to_out)
    pivot(prow, prow, to_mine(1))
    for p in range(PANELS):
        floads[p].wait()

    for d in range(1, R):
        rhs_arrived(0, d).wait_recv()
    solve(0)
    a_hi, a_lo = halves(fbuf0[0:slots].reshape(prow, PANEL))
    mine[1] = mine[1] - product(a_hi, a_lo, ycat[...]).reshape(slots, CYC, cols)
    send_rhs(1)
    tri_forward(1)
    update_rest(0)
    owns[1].wait()
    tri_wait(1)
    invert(1)
    for d in range(1, R):
        rhs_arrived(1, d).wait_recv()
    solve(1)
    update_rest(1)

    @pl.when(me < R - 1)
    def _():
        halo_up().wait_send()

    @pl.when(me > 0)
    def _():
        halo_down().wait_send()

    for p in range(PANELS):
        tri_drain(p)
        for d in range(1, R):
            rhs_copy(p, d).wait_send()
    for k in range(nb):
        for d in range(1, R):
            a2a_copy(k, d).wait_send()


def scale_pivots(values, sizes_here, diag_here, off_here):
    paired = values.reshape(-1, 2, values.shape[1])
    leading = paired[:, 0]
    trailing = paired[:, 1]
    diag_lead = diag_here[0::2][:, None]
    diag_next = diag_here[1::2][:, None]
    coupling = off_here[:, None]
    determ = diag_lead * diag_next - coupling * coupling
    is_pair = (sizes_here == 2)[:, None]
    new_lead = jnp.where(
        is_pair, (diag_next * leading - coupling * trailing) / determ, leading / diag_lead
    )
    new_next = jnp.where(
        is_pair, (diag_lead * trailing - coupling * leading) / determ, trailing / diag_next
    )
    return jnp.stack([new_lead, new_next], axis=1).reshape(values.shape)


def local(vectors, intersection, factor, pivot_rows, pivot_sizes, pivot_diag, pivot_off):
    R = lax.axis_size("row")
    V = lax.axis_size("vec")
    device = lax.axis_index("row")
    rows, cols = vectors.shape
    slots = PANEL // R // CYC
    prow = slots * CYC
    nb = rows // BS
    blocks = rows // CYC
    dma = pltpu.SemaphoreType.DMA
    anywhere = pl.BlockSpec(memory_space=pl.ANY)
    raw = pl.pallas_call(
        functools.partial(kernel, R, V),
        out_shape=jax.ShapeDtypeStruct((rows, cols), F32),
        in_specs=[pl.BlockSpec(memory_space=pltpu.SMEM), anywhere, anywhere, anywhere],
        out_specs=pl.BlockSpec(memory_space=pltpu.VMEM),
        scratch_shapes=[
            pltpu.VMEM(intersection.shape, F32),
            pltpu.VMEM((blocks - slots, CYC, PANEL), F32),
            pltpu.VMEM((blocks - 2 * slots, CYC, PANEL), F32),
            pltpu.VMEM((rows, cols), F32),
            pltpu.VMEM((2, BS, cols), F32),
            pltpu.VMEM((rows + 2 * BS, 2 * cols), BF),
            pltpu.VMEM((R, rows // R, cols), F32),
            pltpu.VMEM((rows, cols), F32),
            pltpu.VMEM((PANELS, slots, CYC, cols), F32),
            pltpu.VMEM((PANELS, slots, R, CYC, cols), F32),
            pltpu.VMEM((PANELS, slots, R, CYC, PANEL), F32),
            pltpu.VMEM((PANEL // STEP, STEP, STEP), BF),
            pltpu.VMEM((PANEL // STEP, STEP, STEP), BF),
            pltpu.VMEM((PANELS, slots, R, CYC, cols), F32),
            pltpu.VMEM((PANEL, 2 * cols), BF),
            dma, dma((nb,)), dma((PANELS,)), dma((PANELS,)),
            dma((2,)), dma((2,)),
            dma((nb, R)), dma((nb, R)), dma((nb,)),
            dma((PANELS, R)), dma((PANELS, R)),
            dma((PANELS, R, V)), dma((PANELS, R, V)),
            dma((PANELS, R)), dma((PANELS, R)),
        ],
        compiler_params=pltpu.CompilerParams(
            collective_id=0, has_side_effects=True, vmem_limit_bytes=62 * 1024 * 1024),
    )(pivot_rows, vectors, intersection, factor.reshape(blocks, CYC, factor.shape[1]))
    pairs = CYC // 2

    def own(x, width):
        x = x.reshape(PANELS * slots, R, width)
        return lax.dynamic_slice_in_dim(x, device, 1, 1).reshape(-1)

    scaled = scale_pivots(
        raw[: PANELS * prow], own(pivot_sizes, pairs), own(pivot_diag, CYC), own(pivot_off, pairs))
    return jnp.concatenate([scaled, raw[PANELS * prow :]], axis=0)


def solution(mesh):
    in_specs = (
        P(("cuts", "row"), "vec"),
        P("row", None),
        P(("cuts", "row"), None),
        P(("cuts", "row")),
        P("cuts"),
        P("cuts"),
        P("cuts"),
    )
    out_specs = P(("cuts", "row"), "vec")
    return jax.shard_map(local, mesh=mesh, in_specs=in_specs, out_specs=out_specs, check_vma=False)
```

```python
import functools
import math

import jax
import jax.numpy as jnp
from jax import lax
from jax.experimental import pallas as pl
from jax.experimental.pallas import tpu as pltpu
from jax.sharding import PartitionSpec as P

BS = 512
SOLVED = 2048
PANEL = 512
PANELS = SOLVED // PANEL
CYC = 16
INV = 128
STEP = 256

MESH = pl.DeviceIdType.MESH
BF = jnp.bfloat16
F32 = jnp.float32


def halves(x):
    hi = x.astype(BF)
    return hi, (x - hi.astype(F32)).astype(BF)


def dot(a, b):
    return jnp.dot(a, b, preferred_element_type=F32)


def product(a_hi, a_lo, b_cat):
    n = b_cat.shape[1] // 2
    wide = dot(a_hi, b_cat)
    return wide[:, :n] + (wide[:, n:] + dot(a_lo, b_cat[:, :n]))


def mm(a, b):
    a_hi, a_lo = halves(a)
    return product(a_hi, a_lo, jnp.concatenate(halves(b), axis=1))


def invert_many(blocks):
    n = blocks[0].shape[0]
    row = lax.broadcasted_iota(jnp.int32, (n, n), 0)
    col = lax.broadcasted_iota(jnp.int32, (n, n), 1)
    strict = col < row
    eye = jnp.where(col == row, 1.0, 0.0).astype(F32)
    small = 16
    base = strict & (row // small == col // small)
    powers = [jnp.where(base, d, 0.0) for d in blocks]
    inv = [eye - m for m in powers]
    reach = 2
    while reach < small:
        powers = [mm(m, m) for m in powers]
        inv = [x + mm(x, m) for x, m in zip(inv, powers)]
        reach *= 2
    size = small
    while size < n:
        joined = strict & (row // (2 * size) == col // (2 * size)) & (row // size != col // size)
        mid = [mm(jnp.where(joined, d, 0.0), x) for d, x in zip(blocks, inv)]
        inv = [x - mm(x, m) for x, m in zip(inv, mid)]
        size *= 2
    return inv


def kernel(
    R, V, piv, sizes, diag, off, vec_hbm, int_hbm, fac_hbm, out,
    ibuf, fbufs, vbuf, halo, bcat, prod, reg, mine, rhs, lbuf, xhi, xlo, ybuf, ycat, alpha, beta,
    in_sem, int_sem, fac_sem, own_sem,
    halo_s, halo_r, a2a_s, a2a_r, a2a_l, tri_s, tri_r, fwd_s, fwd_r, rhs_s, rhs_r,
):
    me = lax.axis_index("row")
    lane = lax.axis_index("vec")
    rows, cols = vbuf.shape
    nb = rows // BS
    slots = PANEL // R // CYC
    prow = slots * CYC
    per_owner = rows // R
    block_share = BS // R
    quarter = PANEL // V
    facs = fbufs

    def quarter_of(v):
        order = []
        lo, hi = 0, V - 1
        while lo <= hi:
            order.append(lo)
            if hi > lo:
                order.append(hi)
            lo, hi = lo + 1, hi - 1
        return order[v]

    def rpeer(d):
        return lax.rem(me + d, R)

    def rfrom(d):
        return lax.rem(me + (R - d), R)

    def vpeer(d):
        return lax.rem(lane + d, V)

    vload = pltpu.make_async_copy(vec_hbm, vbuf, in_sem)
    vload.start()
    order = list(range(1, nb - 1)) + [0, nb - 1]
    iloads = {}
    for k in order:
        iloads[k] = pltpu.make_async_copy(
            int_hbm.at[pl.ds(k * BS, BS)], ibuf.at[pl.ds(k * BS, BS)], int_sem.at[k])
        iloads[k].start()

    barrier = pltpu.get_barrier_semaphore()
    for d in range(1, R):
        pl.semaphore_signal(barrier, 1, device_id={"row": rpeer(d)}, device_id_type=MESH)
    for d in range(1, V):
        pl.semaphore_signal(barrier, 1, device_id={"vec": vpeer(d)}, device_id_type=MESH)
    pl.semaphore_wait(barrier, R - 1 + V - 1)

    def halo_up():
        return pltpu.make_async_remote_copy(
            vec_hbm.at[pl.ds(rows - BS, BS)], halo.at[0], halo_s.at[0], halo_r.at[0],
            device_id={"row": rpeer(1)}, device_id_type=MESH)

    def halo_down():
        return pltpu.make_async_remote_copy(
            vec_hbm.at[pl.ds(0, BS)], halo.at[1], halo_s.at[1], halo_r.at[1],
            device_id={"row": rfrom(1)}, device_id_type=MESH)

    @pl.when(me < R - 1)
    def _():
        halo_up().start()

    @pl.when(me > 0)
    def _():
        halo_down().start()

    def tri_span(v):
        q = quarter_of(v)
        first = (q * quarter) // (R * CYC)
        return q, first, slots - first

    def tri_copy(p, v, d):
        q, first, count = tri_span(v)
        src = fac_hbm.at[pl.ds(p * slots + first, count), :, pl.ds(p * PANEL + q * quarter, quarter)]
        dst = lbuf.at[p, pl.ds(first, count), me, :, pl.ds(q * quarter, quarter)]
        return pltpu.make_async_remote_copy(
            src, dst, tri_s.at[p, d], tri_r.at[p, d],
            device_id={"row": rpeer(d)}, device_id_type=MESH)

    def tri_arrived(p, v, d):
        q, first, count = tri_span(v)
        dst = lbuf.at[p, pl.ds(first, count), rfrom(d), :, pl.ds(q * quarter, quarter)]
        return pltpu.make_async_remote_copy(
            dst, dst, tri_s.at[p, d], tri_r.at[p, d],
            device_id={"row": rpeer(d)}, device_id_type=MESH)

    def fwd_copy(p, v, d, w):
        q, first, count = tri_span(v)
        ref = lbuf.at[p, pl.ds(first, count), rfrom(d), :, pl.ds(q * quarter, quarter)]
        return pltpu.make_async_remote_copy(
            ref, ref, fwd_s.at[p, d, w], fwd_r.at[p, d, v],
            device_id={"vec": (v + w) % V}, device_id_type=MESH)

    def per_lane(fn):
        for v in range(V):
            @pl.when(lane == v)
            def _():
                fn(v)

    def tri_start(p):
        def go(v):
            for d in range(1, R):
                tri_copy(p, v, d).start()
        per_lane(go)

    def tri_forward(p):
        def go(v):
            for d in range(1, R):
                tri_arrived(p, v, d).wait_recv()
                for w in range(1, V):
                    fwd_copy(p, v, d, w).start()
        per_lane(go)

    def tri_wait(p):
        def go(v):
            for d in range(1, R):
                for w in range(1, V):
                    fwd_copy(p, (v + w) % V, d, 1).wait_recv()
        per_lane(go)

    def tri_drain(p):
        def go(v):
            for d in range(1, R):
                tri_copy(p, v, d).wait_send()
                for w in range(1, V):
                    fwd_copy(p, v, d, w).wait_send()
        per_lane(go)

    tri_start(0)
    tri_start(1)

    owns = []
    for p in range(PANELS):
        c = pltpu.make_async_copy(
            fac_hbm.at[pl.ds(p * slots, slots), :, pl.ds(p * PANEL, PANEL)],
            lbuf.at[p, :, me], own_sem.at[p])
        c.start()
        owns.append(c)
    floads = []
    for p in range(PANELS):
        first = (p + 1) * slots
        c = pltpu.make_async_copy(
            fac_hbm.at[pl.ds(first, rows // CYC - first), :, pl.ds(p * PANEL, PANEL)],
            facs[p], fac_sem.at[p])
        c.start()
        floads.append(c)

    def put_cat(at, value):
        hi, lo = halves(value)
        bcat[at : at + value.shape[0], :cols] = hi
        bcat[at : at + value.shape[0], cols:] = lo

    vload.wait()
    for k in range(nb):
        put_cat(BS + k * BS, vbuf[k * BS : (k + 1) * BS])

    tile = STEP

    def a2a_copy(k, d):
        return pltpu.make_async_remote_copy(
            prod.at[rpeer(d), pl.ds(k * block_share, block_share)],
            reg.at[pl.ds(me * per_owner + k * block_share, block_share)],
            a2a_s.at[k, d], a2a_r.at[k, d],
            device_id={"row": rpeer(d)}, device_id_type=MESH)

    def a2a_own(k):
        return pltpu.make_async_copy(
            prod.at[me, pl.ds(k * block_share, block_share)],
            reg.at[pl.ds(me * per_owner + k * block_share, block_share)],
            a2a_l.at[k])

    def a2a_arrived(k, d):
        return pltpu.make_async_remote_copy(
            prod.at[rpeer(d), pl.ds(k * block_share, block_share)],
            reg.at[pl.ds(rfrom(d) * per_owner + k * block_share, block_share)],
            a2a_s.at[k, d], a2a_r.at[k, d],
            device_id={"row": rpeer(d)}, device_id_type=MESH)

    def band(k):
        iloads_wait(k)
        window = bcat[pl.ds(pl.multiple_of(k * BS, BS), 3 * BS), :]
        for t in range(0, BS, tile):
            a = ibuf[pl.ds(pl.multiple_of(k * BS + t, tile), tile), :]
            a_hi, a_lo = halves(a)
            value = product(a_hi, a_lo, window)
            for g in range(tile // CYC):
                number = t // CYC + g
                owner, slot = number % R, number // R
                at = pl.multiple_of(k * block_share + slot * CYC, CYC)
                prod[owner, pl.ds(at, CYC), :] = value[g * CYC : (g + 1) * CYC]
        for d in range(1, R):
            a2a_copy(k, d).start()
        a2a_own(k).start()

    def iloads_wait(k):
        at = pl.multiple_of(k * BS, BS)
        pltpu.make_async_copy(
            int_hbm.at[pl.ds(at, BS)], ibuf.at[pl.ds(at, BS)], int_sem.at[k]).wait()

    pl.loop(1, nb - 1)(band)

    @pl.when(me > 0)
    def _():
        halo_up().wait_recv()
        put_cat(0, halo[0])

    @pl.when(me == 0)
    def _():
        bcat[0:BS, :] = jnp.zeros((BS, 2 * cols), BF)

    @pl.when(me < R - 1)
    def _():
        halo_down().wait_recv()
        put_cat(BS + rows, halo[1])

    @pl.when(me == R - 1)
    def _():
        bcat[BS + rows : 2 * BS + rows, :] = jnp.zeros((BS, 2 * cols), BF)

    @pl.loop(0, 2)
    def _(i):
        band(i * (nb - 1))

    def lrows(p, at, count, c0, c1):
        span = R * CYC
        if count % span == 0:
            value = lbuf[p, at // span : (at + count) // span, :, :, c0:c1]
        else:
            first = at % span // CYC
            value = lbuf[p, at // span, first : first + count // CYC, :, c0:c1]
        return value.reshape(count, c1 - c0)

    per_panel = PANEL // STEP

    def invert(p):
        blocks = [lrows(p, at, INV, at, at + INV) for at in range(0, PANEL, INV)]
        inv = invert_many(blocks)
        for j in range(per_panel):
            first, second = inv[2 * j], inv[2 * j + 1]
            corner = lrows(p, j * STEP + INV, INV, j * STEP, j * STEP + INV)
            corner = -mm(second, mm(corner, first))
            for r0, c0, value in ((0, 0, first), (INV, 0, corner), (INV, INV, second)):
                hi, lo = halves(value)
                xhi[p * per_panel + j, r0 : r0 + INV, c0 : c0 + INV] = hi
                xlo[p * per_panel + j, r0 : r0 + INV, c0 : c0 + INV] = lo
            xhi[p * per_panel + j, 0:INV, INV:STEP] = jnp.zeros((INV, INV), BF)
            xlo[p * per_panel + j, 0:INV, INV:STEP] = jnp.zeros((INV, INV), BF)

    def coefficients():
        sub = lax.broadcasted_iota(jnp.int32, (8, cols), 0)

        @pl.loop(0, PANELS * prow // 8)
        def _(i):
            base = (i // 2 * R + me) * CYC + i % 2 * 8
            own = jnp.zeros((8, cols), F32)
            other = own
            coupling = own
            kind = jnp.zeros((8, cols), jnp.int32)
            for j in range(8):
                here = sub == j
                own = jnp.where(here, diag[base + j], own)
                other = jnp.where(here, diag[base + (j ^ 1)], other)
                if j % 2 == 0:
                    pair = sub // 2 == j // 2
                    coupling = jnp.where(pair, off[base // 2 + j // 2], coupling)
                    kind = jnp.where(pair, sizes[base // 2 + j // 2], kind)
            determ = own * other - coupling * coupling
            two = kind == 2
            at = pl.ds(pl.multiple_of(i * 8, 8), 8)
            alpha[at, :] = jnp.where(two, other / determ, 1.0 / own)
            beta[at, :] = jnp.where(two, -coupling / determ, 0.0)

    def pivot(first, count, store):
        @pl.loop(0, count // 8)
        def _(i):
            picked = [reg[pl.ds(piv[first + i * 8 + j], 1), :] for j in range(8)]
            store(i, jnp.concatenate(picked, axis=0))

    def rhs_copy(p, d):
        return pltpu.make_async_remote_copy(
            mine.at[p], rhs.at[p, :, me], rhs_s.at[p, d], rhs_r.at[p, d],
            device_id={"row": rpeer(d)}, device_id_type=MESH)

    def rhs_arrived(p, d):
        return pltpu.make_async_remote_copy(
            mine.at[p], rhs.at[p, :, rfrom(d)], rhs_s.at[p, d], rhs_r.at[p, d],
            device_id={"row": rpeer(d)}, device_id_type=MESH)

    def send_rhs(p):
        for d in range(1, R):
            rhs_copy(p, d).start()
        rhs[p, :, pl.ds(me, 1)] = mine[p].reshape(slots, 1, CYC, cols)

    def blockrows(ref, p, at, count):
        span = R * CYC
        if count % span == 0:
            return ref.at[p, at // span : (at + count) // span]
        first = at % span // CYC
        return ref.at[p, at // span, first : first + count // CYC]

    def solve(p):
        for i in range(PANEL // STEP):
            at = i * STEP
            acc = blockrows(rhs, p, at, STEP)[...].reshape(STEP, cols)
            if i > 0:
                l_hi, l_lo = halves(lrows(p, at, STEP, 0, at))
                acc = acc - product(l_hi, l_lo, ycat[:at])
            y = product(xhi[p * per_panel + i], xlo[p * per_panel + i], jnp.concatenate(halves(acc), axis=1))
            target = blockrows(ybuf, p, at, STEP)
            target[...] = y.reshape(target.shape)
            hi, lo = halves(y)
            ycat[at : at + STEP, :cols] = hi
            ycat[at : at + STEP, cols:] = lo

    def scale(p):
        y = ybuf[p, :, pl.ds(me, 1)].reshape(prow, cols)
        row = lax.broadcasted_iota(jnp.int32, (prow, cols), 0)
        other = jnp.where(row % 2 == 0, pltpu.roll(y, prow - 1, 0), pltpu.roll(y, 1, 0))
        at = slice(p * prow, (p + 1) * prow)
        out[at, :] = alpha[at, :] * y + beta[at, :] * other

    rest = rows - PANELS * prow

    def subtract(p, first, count):
        f = facs[p]
        part = math.gcd(count, STEP)
        skip = first // CYC - (p + 1) * slots

        @pl.loop(0, count // part)
        def _(t):
            at = pl.multiple_of(first + t * part, CYC)
            a = f[pl.ds(skip + t * (part // CYC), part // CYC)].reshape(part, PANEL)
            a_hi, a_lo = halves(a)
            out[pl.ds(at, part), :] = out[pl.ds(at, part), :] - product(a_hi, a_lo, ycat[...])

    def to_out(first):
        def store(i, value):
            out[pl.ds(pl.multiple_of(first + i * 8, 8), 8), :] = value
        return store

    def to_mine(i, value):
        mine[0, i // 2, pl.ds(pl.multiple_of(i % 2 * 8, 8), 8), :] = value

    def ready(p):
        owns[p].wait()
        tri_wait(p)
        invert(p)

    tri_forward(0)
    coefficients()
    tri_forward(1)
    ready(0)
    ready(1)

    for k in range(nb):
        for d in range(1, R):
            a2a_arrived(k, d).wait_recv()
        a2a_own(k).wait()

    pivot(0, prow, to_mine)
    send_rhs(0)
    for p in range(2, PANELS):
        tri_start(p)
    pivot(prow, rows - prow, to_out(prow))
    for p in range(PANELS):
        floads[p].wait()

    for p in range(PANELS):
        for d in range(1, R):
            rhs_arrived(p, d).wait_recv()
        solve(p)
        if p + 1 < PANELS:
            at = (p + 1) * prow
            a_hi, a_lo = halves(facs[p][0:slots].reshape(prow, PANEL))
            value = out[at : at + prow, :] - product(a_hi, a_lo, ycat[...])
            mine[p + 1] = value.reshape(slots, CYC, cols)
            send_rhs(p + 1)
        if p == 0:
            for n in range(2, PANELS):
                tri_forward(n)
        scale(p)
        if p + 2 < PANELS:
            subtract(p, (p + 2) * prow, (PANELS - p - 2) * prow)
        subtract(p, PANELS * prow, rest)
        if p + 2 < PANELS:
            ready(p + 2)

    @pl.when(me < R - 1)
    def _():
        halo_up().wait_send()

    @pl.when(me > 0)
    def _():
        halo_down().wait_send()

    for p in range(PANELS):
        tri_drain(p)
        for d in range(1, R):
            rhs_copy(p, d).wait_send()
    for k in range(nb):
        for d in range(1, R):
            a2a_copy(k, d).wait_send()


def local(vectors, intersection, factor, pivot_rows, pivot_sizes, pivot_diag, pivot_off):
    R = lax.axis_size("row")
    V = lax.axis_size("vec")
    rows, cols = vectors.shape
    slots = PANEL // R // CYC
    prow = slots * CYC
    nb = rows // BS
    blocks = rows // CYC
    dma = pltpu.SemaphoreType.DMA
    anywhere = pl.BlockSpec(memory_space=pl.ANY)
    smem = pl.BlockSpec(memory_space=pltpu.SMEM)
    return pl.pallas_call(
        functools.partial(kernel, R, V),
        out_shape=jax.ShapeDtypeStruct((rows, cols), F32),
        in_specs=[smem] * 4 + [anywhere] * 3,
        out_specs=pl.BlockSpec(memory_space=pltpu.VMEM),
        scratch_shapes=[
            pltpu.VMEM(intersection.shape, F32),
            [pltpu.VMEM((blocks - (p + 1) * slots, CYC, PANEL), F32) for p in range(PANELS)],
            pltpu.VMEM((rows, cols), F32),
            pltpu.VMEM((2, BS, cols), F32),
            pltpu.VMEM((rows + 2 * BS, 2 * cols), BF),
            pltpu.VMEM((R, rows // R, cols), F32),
            pltpu.VMEM((rows, cols), F32),
            pltpu.VMEM((PANELS, slots, CYC, cols), F32),
            pltpu.VMEM((PANELS, slots, R, CYC, cols), F32),
            pltpu.VMEM((PANELS, slots, R, CYC, PANEL), F32),
            pltpu.VMEM((SOLVED // STEP, STEP, STEP), BF),
            pltpu.VMEM((SOLVED // STEP, STEP, STEP), BF),
            pltpu.VMEM((PANELS, slots, R, CYC, cols), F32),
            pltpu.VMEM((PANEL, 2 * cols), BF),
            pltpu.VMEM((PANELS * prow, cols), F32),
            pltpu.VMEM((PANELS * prow, cols), F32),
            dma, dma((nb,)), dma((PANELS,)), dma((PANELS,)),
            dma((2,)), dma((2,)),
            dma((nb, R)), dma((nb, R)), dma((nb,)),
            dma((PANELS, R)), dma((PANELS, R)),
            dma((PANELS, R, V)), dma((PANELS, R, V)),
            dma((PANELS, R)), dma((PANELS, R)),
        ],
        compiler_params=pltpu.CompilerParams(
            collective_id=0, has_side_effects=True, vmem_limit_bytes=62 * 1024 * 1024),
    )(pivot_rows, pivot_sizes, pivot_diag, pivot_off, vectors, intersection,
      factor.reshape(blocks, CYC, factor.shape[1]))


def solution(mesh):
    in_specs = (
        P(("cuts", "row"), "vec"),
        P("row", None),
        P(("cuts", "row"), None),
        P(("cuts", "row")),
        P("cuts"),
        P("cuts"),
        P("cuts"),
    )
    out_specs = P(("cuts", "row"), "vec")
    return jax.shard_map(local, mesh=mesh, in_specs=in_specs, out_specs=out_specs, check_vma=False)
```
